32 devices in a mesh: dp: 8 (over y, x, core), tensor: 4 (over z).
Axes of the slice: x: 2, y: 2, z: 4, core: 2. Of those that a mesh axis runs over, the one named last changes fastest.
Arguments:
- acts: bfloat16 [3072, 4096], P('dp', 'tensor'), may hold values from -6 to 6
- grad_out: bfloat16 [3072, 4096], P('dp', 'tensor'), may hold values from -60 to 60
- gate_pre: bfloat16 [3072, 14336], P('dp', 'tensor'), may hold values from -6 to 6
- up_pre: bfloat16 [3072, 14336], P('dp', 'tensor'), may hold values from -6 to 6
- down_weight: bfloat16 [14336, 4096], P('tensor', 'dp'), may hold values from -0.09375 to 0.09375
- proj_in: bfloat16 [4096, 64], P('tensor'), may hold values from -0.09375 to 0.09375
- proj_out: bfloat16 [14336, 64], P('tensor'), may hold values from -0.046875 to 0.046875
- lengths: int32 [24], P('dp'), may hold values from 64 to 128
- query_ids: int32 [16], replicated, may hold values from 0 to 23
Outputs:
- gram: float32 [4096, 4096], P('dp', 'tensor')
- scores: float32 [16, 24], P(None, 'dp')
The draws below stay inside these ranges and needn't reach their ends.
Inputs may be any that keep to these rules, and one draw needn't show every extreme that they name: `query_ids`: queries may repeat.
All inputs are finite; a program needn't handle non-finite values.
Results may differ from the reference program's by a relative error of at most 0.004.
Values may be sent and summed in bfloat16 or wider, within the bound.
A program may use at most 128 MiB of HBM per device.

```python
import jax
import jax.numpy as jnp
from jax import lax

D = 4096
FF = 14336
KI = 64
KO = 64
SEQ = 128
Q = 16
EXAMPLES = 24
TOKENS = 3072
FEAT = 4096


def draw_grad_out(key, part):
    key = jax.random.fold_in(key, 101)
    total_rows = EXAMPLES * SEQ
    example = jnp.arange(total_rows) // SEQ
    ramp = example.astype(jnp.float32) / EXAMPLES
    values = jnp.clip(jax.random.normal(key, (total_rows, D), jnp.float32), -6.0, 6.0)
    factor = jnp.power(10.0, ramp)
    return (values * factor[:, None]).astype(jnp.bfloat16)


def draw_acts(key, part):
    key = jax.random.fold_in(key, 202)
    total_rows = EXAMPLES * SEQ
    values = jnp.clip(jax.random.normal(key, (total_rows, D), jnp.float32), -6.0, 6.0)
    return values.astype(jnp.bfloat16)


def draw_up_pre(key, part):
    key = jax.random.fold_in(key, 303)
    total_rows = EXAMPLES * SEQ
    values = jnp.clip(jax.random.normal(key, (total_rows, FF), jnp.float32), -6.0, 6.0)
    return values.astype(jnp.bfloat16)


def with_ends(entries, key, least, largest):
    index_at = [jax.random.randint(jax.random.fold_in(key, axis), (), 0, length) for axis, length in enumerate(entries.shape)]
    widest = entries.shape.index(max(entries.shape))
    neighbour = index_at[:widest] + [(index_at[widest] + 1) % entries.shape[widest]] + index_at[widest + 1:]
    return entries.at[tuple(index_at)].set(least).at[tuple(neighbour)].set(largest)


def level_of(own_key, shape, cuts, low, high):
    gain, own = 1.0, jax.random.fold_in(own_key, 6)
    for position, shards_of in cuts:
        steps = jnp.exp(jax.random.uniform(jax.random.fold_in(own, position), (shards_of,), jnp.float32, low / len(cuts), high / len(cuts)))
        gain = gain * jnp.repeat(steps, shape[position] // shards_of).reshape([-1 if axis == position else 1 for axis in range(len(shape))])
    return gain


def centred(stream_key, shape, width, bound, cuts=(), held_as=jnp.bfloat16):
    values = jax.random.normal(stream_key, shape, jnp.float32) * width
    if len(cuts) > 0:
        values = level_of(stream_key, shape, cuts, -0.22, 0.18) * values
    return jnp.clip(values, min=-bound, max=bound).astype(held_as)


def setup_inputs(seed: int = 0) -> dict:
    streams_of = jax.random.split(jax.random.key(seed), 10)
    acts = draw_acts(jax.random.fold_in(streams_of[9], 71), 0)
    grad_out = draw_grad_out(jax.random.fold_in(streams_of[9], 71), 0)
    gate_pre = centred(streams_of[2], (TOKENS, FF), 1.0, 6.0, ((0, 8), (1, 4)))
    up_pre = draw_up_pre(jax.random.fold_in(streams_of[9], 71), 0)
    down_weight = centred(streams_of[4], (FF, D), D ** -0.5, 0.09375, ((0, 4), (1, 8)))
    proj_in = centred(streams_of[5], (D, KI), D ** -0.5, 0.09375, ((0, 4),))
    proj_out = centred(streams_of[6], (FF, KO), FF ** -0.5, 0.046875, ((0, 4),))
    lengths = with_ends(jax.random.randint(streams_of[7], (EXAMPLES,), SEQ // 2, SEQ + 1), jax.random.fold_in(streams_of[7], 1), SEQ // 2, SEQ).astype(jnp.int32)
    query_ids = with_ends(jax.random.randint(streams_of[8], (Q,), 0, EXAMPLES), jax.random.fold_in(streams_of[8], 1), 0, EXAMPLES - 1).astype(jnp.int32)
    return {"acts": acts, "grad_out": grad_out, "gate_pre": gate_pre, "up_pre": up_pre, "down_weight": down_weight, "proj_in": proj_in, "proj_out": proj_out, "lengths": lengths, "query_ids": query_ids}


def silu_slope(value):
    sigma = jax.nn.sigmoid(value)
    return sigma + value * sigma * (1.0 - sigma)


def reference(acts, grad_out, gate_pre, up_pre, down_weight, proj_in, proj_out, lengths, query_ids):
    highest = lax.Precision.HIGHEST
    weight_full = down_weight.astype(jnp.float32)

    def one_example(items):
        act_rows, grad_rows, gate_rows, up_rows, length = items
        hidden_grad = jnp.dot(grad_rows.astype(jnp.float32), weight_full.T, precision=highest)
        gate_value = gate_rows.astype(jnp.float32)
        gate_grad = (hidden_grad * up_rows.astype(jnp.float32) * silu_slope(gate_value)).astype(jnp.bfloat16)
        out_factor = jnp.dot(gate_grad, proj_out, preferred_element_type=jnp.float32)
        in_factor = jnp.dot(act_rows, proj_in, preferred_element_type=jnp.float32)
        live = (jnp.arange(SEQ, dtype=jnp.int32) < length).astype(jnp.float32)
        out_factor = out_factor * live[:, None]
        return jnp.dot(out_factor.T, in_factor, precision=highest).reshape(-1)

    features = lax.map(one_example, (acts.reshape(EXAMPLES, SEQ, D), grad_out.reshape(EXAMPLES, SEQ, D),
                                     gate_pre.reshape(EXAMPLES, SEQ, FF), up_pre.reshape(EXAMPLES, SEQ, FF), lengths))
    norm_mean = jnp.sum(features * features) / EXAMPLES + 1e-6
    gram = jnp.dot(features.T, features, precision=highest) * (FEAT / EXAMPLES) / norm_mean
    query_feat = features[query_ids]
    scores = jnp.dot(query_feat, features.T, precision=highest) / norm_mean
    return gram, scores
```

```python
import functools

import jax
import jax.numpy as jnp
from jax import lax
from jax.experimental import pallas as pl
from jax.experimental.pallas import tpu as pltpu
from jax.sharding import PartitionSpec as P

MESH = pl.DeviceIdType.MESH
HIGHEST = lax.Precision.HIGHEST
LANES = 128
PIECES = 7


def dot_nt(a, b, precision=None):
    return lax.dot_general(
        a, b, (((1,), (1,)), ((), ())), preferred_element_type=jnp.float32, precision=precision
    )


def kernel(
    n, nt,
    acts, grad, gate, up, weight, proj_in, proj_out, lengths, query_ids,
    gram, scores,
    wbuf, gbuf, gate_v, up_v, acts_v, pin_v, pout_v, pin_t, pout_t,
    acc, oacc, orecv, iacc, irecv, inpad, fbuf, cols, kbuf, rbuf, lhs_s, rhs_s,
    local_sem, w_send, w_recv, s_send, s_recv, g_send, g_recv, i_send, i_recv,
    o_send, o_recv, f_send, f_recv, k_send, k_recv, r_send, r_recv,
):
    me = lax.axis_index("dp")
    t = lax.axis_index("tensor")
    chips = n // 2
    half_ring = chips // 2
    chip = me // 2
    core = me % 2
    ff, kw = weight.shape
    tokens, gw = grad.shape
    ex = lengths.shape[0]
    seq = tokens // ex
    ki = proj_in.shape[1]
    ko = proj_out.shape[1]
    tiles = cols.shape[0]
    every = cols.shape[1]
    row_tiles = rbuf.shape[0]
    rows = ff // PIECES
    sibling = chip * 2 + 1 - core

    def step_left(c, s):
        if chips == 4:
            return [c, (3 * c + 2) % 5, 3 - c, (2 * c + 1) % 5][s % 4]
        return (c - s + chips) % chips

    def step_right(c, s):
        return step_left(c, chips - s)

    barrier = pltpu.get_barrier_semaphore()
    for k in range(1, n):
        pl.semaphore_signal(barrier, inc=1, device_id=((me + k) % n, t), device_id_type=MESH)
    for k in range(1, nt):
        pl.semaphore_signal(barrier, inc=1, device_id=(me, (t + k) % nt), device_id_type=MESH)
    pl.semaphore_wait(barrier, n + nt - 2)

    def remote(src, dst, send, recv, dp_id, t_id):
        return pltpu.make_async_remote_copy(
            src_ref=src, dst_ref=dst, send_sem=send, recv_sem=recv,
            device_id=(dp_id, t_id), device_id_type=MESH,
        )

    def span(way, s, p):
        if s < half_ring:
            return pl.ds(pl.multiple_of(p * rows, 32), rows)
        return pl.ds(pl.multiple_of(p * rows + way * (rows // 2), 32), rows // 2)

    def ring_send(way, s, p):
        origin = step_left(chip, s - 1) if way == 0 else step_right(chip, s - 1)
        target = step_right(chip, 1) if way == 0 else step_left(chip, 1)
        slot = origin * 2 + core
        part = span(way, s, p)
        src = weight.at[part] if s == 1 else wbuf.at[slot, part]
        return remote(
            src, wbuf.at[slot, part], w_send.at[way, s - 1, p], w_recv.at[way, s - 1, p],
            target * 2 + core, t,
        )

    def ring_slot(way, s):
        return (step_left(chip, s) if way == 0 else step_right(chip, s)) * 2 + core

    def ring_recv(way, s, p):
        slot = ring_slot(way, s)
        part = span(way, s, p)
        return remote(
            wbuf.at[slot, part], wbuf.at[slot, part],
            w_send.at[way, s - 1, p], w_recv.at[way, s - 1, p], sibling, t,
        )

    def sib_send(way, s, p):
        if s == 0:
            part = span(0, 0, p)
            return remote(
                weight.at[part], wbuf.at[me, part], s_send.at[0, p], s_recv.at[0, p], sibling, t
            )
        slot = ring_slot(way, s)
        part = span(way, s, p)
        at = 1 + way * half_ring + s - 1
        return remote(
            wbuf.at[slot, part], wbuf.at[slot, part], s_send.at[at, p], s_recv.at[at, p], sibling, t
        )

    def sib_recv(way, s, p):
        if s == 0:
            slot, at, part = sibling, 0, span(0, 0, p)
        else:
            slot = ring_slot(way, s) - core + 1 - core
            at = 1 + way * half_ring + s - 1
            part = span(way, s, p)
        return remote(
            wbuf.at[slot, part], wbuf.at[slot, part], s_send.at[at, p], s_recv.at[at, p], sibling, t
        )

    @pl.loop(0, PIECES)
    def _(p):
        ring_send(0, 1, p).start()
        ring_send(1, 1, p).start()

    def grad_copy(k):
        return remote(
            grad, gbuf.at[t], g_send.at[k], g_recv.at[k], me, (t + k) % nt
        )

    def grad_recv(k):
        src = (t - k + nt) % nt
        return remote(grad, gbuf.at[src], g_send.at[k], g_recv.at[k], me, (t + k) % nt)

    for k in range(1, nt):
        grad_copy(k).start()

    locals_ = [
        pltpu.make_async_copy(acts, acts_v, local_sem.at[0]),
        pltpu.make_async_copy(proj_in, pin_v, local_sem.at[1]),
        pltpu.make_async_copy(proj_out, pout_v, local_sem.at[2]),
        pltpu.make_async_copy(weight, wbuf.at[me], local_sem.at[3]),
        pltpu.make_async_copy(gate, gate_v, local_sem.at[4]),
        pltpu.make_async_copy(up, up_v, local_sem.at[5]),
        pltpu.make_async_copy(grad, gbuf.at[t], local_sem.at[6]),
    ]
    for copy in locals_:
        copy.start()

    @pl.loop(0, PIECES)
    def _(p):
        sib_send(0, 0, p).start()

    locals_[0].wait()
    locals_[1].wait()
    row_id = lax.broadcasted_iota(jnp.int32, (ki, ki), 0)
    col_id = lax.broadcasted_iota(jnp.int32, (ki, ki), 1)
    pin_t[...] = dot_nt((row_id == col_id).astype(jnp.bfloat16), pin_v[...]).astype(jnp.bfloat16)
    iacc[...] = dot_nt(pin_t[...], acts_v[...])

    def in_copy(k):
        return remote(iacc, irecv.at[k - 1], i_send.at[k], i_recv.at[k], me, (t + k) % nt)

    for k in range(1, nt):
        in_copy(k).start()
    locals_[2].wait()
    per_t = ko // nt
    row_id = lax.broadcasted_iota(jnp.int32, (ko, ko), 0)
    col_id = lax.broadcasted_iota(jnp.int32, (ko, ko), 1)
    place = (col_id // per_t) * per_t + (col_id % 2) * tiles + (col_id % per_t) // 2
    pout_t[...] = dot_nt((row_id == place).astype(jnp.bfloat16), pout_v[...]).astype(jnp.bfloat16)
    acc[...] = jnp.zeros_like(acc)
    inpad[...] = jnp.zeros_like(inpad)

    if half_ring > 1:
        @pl.loop(0, PIECES)
        def _(p):
            for s in range(1, half_ring):
                for way in (0, 1):
                    ring_recv(way, s, p).wait_recv()
                    ring_send(way, s + 1, p).start()
                    sib_send(way, s, p).start()

    for copy in locals_[3:]:
        copy.wait()
    for k in range(1, nt):
        grad_recv(k).wait_recv()
        in_copy(k).wait_recv()
    total_in = iacc[...]
    for k in range(1, nt):
        total_in = total_in + irecv[k - 1]
    inpad[0, 0:ki] = total_in
    inpad[1, ki : 2 * ki] = total_in

    @pl.loop(0, PIECES)
    def _(p):
        for way in (0, 1):
            ring_recv(way, half_ring, p).wait_recv()
            sib_send(way, half_ring, p).start()
        sib_recv(0, 0, p).wait_recv()
        for s in range(1, half_ring + 1):
            for way in (0, 1):
                sib_recv(way, s, p).wait_recv()
        here = pl.ds(pl.multiple_of(p * rows, LANES), rows)
        hidden = jnp.zeros((tokens, rows), jnp.float32)
        for j in range(n):
            at = j * kw
            hidden = hidden + dot_nt(
                gbuf[at // gw, :, at % gw : at % gw + kw], wbuf[j, here, :]
            )
        value = gate_v[:, here].astype(jnp.float32)
        sigma = jax.nn.sigmoid(value)
        slope = sigma + value * sigma * (1.0 - sigma)
        grads = (hidden * up_v[:, here].astype(jnp.float32) * slope).astype(jnp.bfloat16)
        acc[...] += dot_nt(pout_t[:, here], grads)

    for tt in range(nt):
        for par in (0, 1):
            first = (tt * 2 + par) * tiles
            oacc[tt, par] = acc[first : first + tiles, :]

    def out_copy(k):
        to = (t + k) % nt
        return remote(oacc.at[to], orecv.at[k - 1], o_send.at[k], o_recv.at[k], me, to)

    for k in range(1, nt):
        out_copy(k).start()
    for k in range(1, nt):
        out_copy(k).wait_recv()
    evens = oacc[t, 0]
    odds = oacc[t, 1]
    for k in range(1, nt):
        evens = evens + orecv[k - 1, 0]
        odds = odds + orecv[k - 1, 1]

    position = lax.broadcasted_iota(jnp.int32, (tiles, seq), 1)
    for e in range(ex):
        live = (position < lengths[e]).astype(jnp.float32)
        own = slice(e * seq, (e + 1) * seq)
        fbuf[me * ex + e] = dot_nt(evens[:, own] * live, inpad[0, :, own], HIGHEST) + dot_nt(
            odds[:, own] * live, inpad[1, :, own], HIGHEST
        )

    def feat_copy(k):
        part = fbuf.at[pl.ds(me * ex, ex)]
        return remote(part, part, f_send.at[k], f_recv.at[k], (me + k) % n, t)

    def feat_recv(k):
        part = fbuf.at[pl.ds(((me - k + n) % n) * ex, ex)]
        return remote(part, part, f_send.at[k], f_recv.at[k], (me + k) % n, t)

    for k in range(1, n):
        feat_copy(k).start()
    for k in range(1, n):
        feat_recv(k).wait_recv()

    for s in range(tiles):
        cols[s] = fbuf[:, s, :]

    owner = (me * row_tiles) // tiles
    offset = (me * row_tiles) % tiles

    def row_copy(k):
        return remote(
            cols.at[pl.ds(offset, row_tiles)], rbuf, r_send.at[k], r_recv, me, (t + k) % nt
        )

    @pl.when(t == owner)
    def _():
        for k in range(1, nt):
            row_copy(k).start()
        rbuf[...] = cols[pl.ds(offset, row_tiles)]

    inner = jnp.zeros((every, every), jnp.float32)
    for s in range(tiles):
        inner = inner + dot_nt(cols[s], cols[s], HIGHEST)
    kbuf[t] = jnp.zeros(kbuf.shape[1:], jnp.float32)
    kbuf[t, :, 0:every] = inner

    def inner_copy(k):
        return remote(kbuf.at[t], kbuf.at[t], k_send.at[k], k_recv.at[k], me, (t + k) % nt)

    def inner_recv(k):
        src = (t - k + nt) % nt
        return remote(kbuf.at[src], kbuf.at[src], k_send.at[k], k_recv.at[k], me, (t + k) % nt)

    for k in range(1, nt):
        inner_copy(k).start()

    for s in range(tiles):
        value = cols[s]
        high = value.astype(jnp.bfloat16).astype(jnp.float32)
        own = slice(s * LANES, (s + 1) * LANES)
        rhs_s[0:every, own] = high
        rhs_s[every : 2 * every, own] = value - high
        rhs_s[2 * every : 3 * every, own] = high
    right = rhs_s[...].astype(jnp.bfloat16)

    for k in range(1, nt):
        inner_recv(k).wait_recv()
    whole = kbuf[0]
    for tt in range(1, nt):
        whole = whole + kbuf[tt]
    whole = whole[:, 0:every]
    r_id = lax.broadcasted_iota(jnp.int32, (every, every), 0)
    c_id = lax.broadcasted_iota(jnp.int32, (every, every), 1)
    norm_mean = jnp.sum(jnp.where(r_id == c_id, whole, 0.0)) / every + 1e-6

    queries = scores.shape[0]
    q_row = lax.broadcasted_iota(jnp.int32, (queries, every), 0)
    q_col = lax.broadcasted_iota(jnp.int32, (queries, every), 1)
    chosen = jnp.zeros((queries, every), jnp.float32)
    for q in range(queries):
        chosen = jnp.where((q_row == q) & (q_col == query_ids[q]), 1.0, chosen)
    picked = jnp.dot(chosen, whole, precision=HIGHEST, preferred_element_type=jnp.float32)
    e_row = lax.broadcasted_iota(jnp.int32, (ex, every), 0)
    e_col = lax.broadcasted_iota(jnp.int32, (ex, every), 1)
    mine = (e_col == e_row + me * ex).astype(jnp.float32)
    scores[...] = dot_nt(picked, mine, HIGHEST) / norm_mean

    @pl.when(t != owner)
    def _():
        row_copy(1).wait_recv()

    for s in range(row_tiles):
        value = rbuf[s]
        high = value.astype(jnp.bfloat16).astype(jnp.float32)
        own = slice(s * LANES, (s + 1) * LANES)
        lhs_s[0:every, own] = high
        lhs_s[every : 2 * every, own] = high
        lhs_s[2 * every : 3 * every, own] = value - high
    scale = (tiles * nt * LANES / every) / norm_mean
    for s in range(row_tiles):
        own = slice(s * LANES, (s + 1) * LANES)
        left = lhs_s[:, own].T.astype(jnp.bfloat16)
        gram[own, :] = jnp.dot(left, right, preferred_element_type=jnp.float32) * scale

    @pl.loop(0, PIECES)
    def _(p):
        sib_send(0, 0, p).wait_send()
        for s in range(1, half_ring + 1):
            for way in (0, 1):
                ring_send(way, s, p).wait_send()
                sib_send(way, s, p).wait_send()

    for k in range(1, nt):
        grad_copy(k).wait_send()
        in_copy(k).wait_send()
        out_copy(k).wait_send()
        inner_copy(k).wait_send()
    for k in range(1, n):
        feat_copy(k).wait_send()

    @pl.when(t == owner)
    def _():
        for k in range(1, nt):
            row_copy(k).wait_send()


def body(n, nt, acts, grad_out, gate_pre, up_pre, down_weight, proj_in, proj_out, lengths, query_ids):
    tokens, gw = grad_out.shape
    ff, kw = down_weight.shape
    ki = proj_in.shape[1]
    ko = proj_out.shape[1]
    ex = lengths.shape[0]
    every = ex * n
    width = ki * ko
    tiles = width // nt // LANES
    row_tiles = width // n // LANES
    half_ring = n // 4
    bf16, f32 = jnp.bfloat16, jnp.float32
    dma = pltpu.SemaphoreType.DMA
    hbm = pl.BlockSpec(memory_space=pl.ANY)
    smem = pl.BlockSpec(memory_space=pltpu.SMEM)
    vmem = pl.BlockSpec(memory_space=pltpu.VMEM)
    return pl.pallas_call(
        functools.partial(kernel, n, nt),
        out_shape=(
            jax.ShapeDtypeStruct((width // n, width // nt), f32),
            jax.ShapeDtypeStruct((query_ids.shape[0], ex), f32),
        ),
        in_specs=[hbm] * 7 + [smem] * 2,
        out_specs=(vmem, vmem),
        scratch_shapes=[
            pltpu.VMEM((n, ff, kw), bf16),
            pltpu.VMEM((nt, tokens, gw), bf16),
            pltpu.VMEM((tokens, ff), bf16),
            pltpu.VMEM((tokens, ff), bf16),
            pltpu.VMEM((tokens, gw), bf16),
            pltpu.VMEM((gw, ki), bf16),
            pltpu.VMEM((ff, ko), bf16),
            pltpu.VMEM((ki, gw), bf16),
            pltpu.VMEM((ko, ff), bf16),
            pltpu.VMEM((ko, tokens), f32),
            pltpu.VMEM((nt, 2, tiles, tokens), f32),
            pltpu.VMEM((nt - 1, 2, tiles, tokens), f32),
            pltpu.VMEM((ki, tokens), f32),
            pltpu.VMEM((nt - 1, ki, tokens), f32),
            pltpu.VMEM((2, 2 * ki, tokens), f32),
            pltpu.VMEM((every, tiles, LANES), f32),
            pltpu.VMEM((tiles, every, LANES), f32),
            pltpu.VMEM((nt, every, LANES), f32),
            pltpu.VMEM((row_tiles, every, LANES), f32),
            pltpu.VMEM((3 * every, row_tiles * LANES), f32),
            pltpu.VMEM((3 * every, tiles * LANES), f32),
            dma((7,)),
            dma((2, half_ring, PIECES)),
            dma((2, half_ring, PIECES)),
            dma((1 + 2 * half_ring, PIECES)),
            dma((1 + 2 * half_ring, PIECES)),
            dma((nt,)), dma((nt,)), dma((nt,)), dma((nt,)), dma((nt,)), dma((nt,)),
            dma((n,)), dma((n,)),
            dma((nt,)), dma((nt,)),
            dma((nt,)), dma,
        ],
        compiler_params=pltpu.CompilerParams(
            collective_id=0, has_side_effects=True, vmem_limit_bytes=60 * 1024 * 1024
        ),
    )(acts, grad_out, gate_pre, up_pre, down_weight, proj_in, proj_out, lengths, query_ids)


def solution(mesh):
    in_specs = (
        P("dp", "tensor"),
        P("dp", "tensor"),
        P("dp", "tensor"),
        P("dp", "tensor"),
        P("tensor", "dp"),
        P("tensor", None),
        P("tensor", None),
        P("dp"),
        P(),
    )
    out_specs = (P("dp", "tensor"), P(None, "dp"))
    return jax.shard_map(
        functools.partial(body, mesh.shape["dp"], mesh.shape["tensor"]),
        mesh=mesh, in_specs=in_specs, out_specs=out_specs, check_vma=False,
    )
```

```python
import functools

import jax
import jax.numpy as jnp
from jax import lax
from jax.experimental import pallas as pl
from jax.experimental.pallas import tpu as pltpu
from jax.sharding import PartitionSpec as P

MESH = pl.DeviceIdType.MESH
HIGHEST = lax.Precision.HIGHEST
LANES = 128
PIECES = 7


def dot_nt(a, b, precision=None):
    return lax.dot_general(
        a, b, (((1,), (1,)), ((), ())), preferred_element_type=jnp.float32, precision=precision
    )


def kernel(
    n, nt,
    acts, grad, gate, up, weight, proj_in, proj_out, lengths,
    cols, rbuf, inner_out,
    wbuf, gbuf, gate_v, up_v, acts_v, pin_v, pout_v, pout_t,
    acc, oacc, orecv, iacc, irecv, inpad, fbuf, kbuf,
    local_sem, w_send, w_recv, s_send, s_recv, g_send, g_recv, i_send, i_recv,
    o_send, o_recv, f_send, f_recv, k_send, k_recv, r_send, r_recv,
):
    me = lax.axis_index("dp")
    t = lax.axis_index("tensor")
    chips = n // 2
    half_ring = chips // 2
    chip = me // 2
    core = me % 2
    ff, kw = weight.shape
    tokens, gw = grad.shape
    ex = lengths.shape[0]
    seq = tokens // ex
    ki = proj_in.shape[0]
    ko = proj_out.shape[0]
    tiles = cols.shape[0]
    every = cols.shape[1]
    row_tiles = rbuf.shape[0]
    rows = ff // PIECES
    sibling = chip * 2 + 1 - core

    def step_left(c, s):
        if chips == 4:
            return [c, (3 * c + 2) % 5, 3 - c, (2 * c + 1) % 5][s % 4]
        return (c - s + chips) % chips

    def step_right(c, s):
        return step_left(c, chips - s)

    barrier = pltpu.get_barrier_semaphore()
    for k in range(1, n):
        pl.semaphore_signal(barrier, inc=1, device_id=((me + k) % n, t), device_id_type=MESH)
    for k in range(1, nt):
        pl.semaphore_signal(barrier, inc=1, device_id=(me, (t + k) % nt), device_id_type=MESH)
    pl.semaphore_wait(barrier, n + nt - 2)

    def remote(src, dst, send, recv, dp_id, t_id):
        return pltpu.make_async_remote_copy(
            src_ref=src, dst_ref=dst, send_sem=send, recv_sem=recv,
            device_id=(dp_id, t_id), device_id_type=MESH,
        )

    def span(way, s, p):
        if s < half_ring:
            return pl.ds(pl.multiple_of(p * rows, 32), rows)
        return pl.ds(pl.multiple_of(p * rows + way * (rows // 2), 32), rows // 2)

    def ring_send(way, s, p):
        origin = step_left(chip, s - 1) if way == 0 else step_right(chip, s - 1)
        target = step_right(chip, 1) if way == 0 else step_left(chip, 1)
        slot = origin * 2 + core
        part = span(way, s, p)
        src = weight.at[part] if s == 1 else wbuf.at[slot, part]
        return remote(
            src, wbuf.at[slot, part], w_send.at[way, s - 1, p], w_recv.at[way, s - 1, p],
            target * 2 + core, t,
        )

    def ring_slot(way, s):
        return (step_left(chip, s) if way == 0 else step_right(chip, s)) * 2 + core

    def ring_recv(way, s, p):
        slot = ring_slot(way, s)
        part = span(way, s, p)
        return remote(
            wbuf.at[slot, part], wbuf.at[slot, part],
            w_send.at[way, s - 1, p], w_recv.at[way, s - 1, p], sibling, t,
        )

    def sib_send(way, s, p):
        if s == 0:
            part = span(0, 0, p)
            return remote(
                weight.at[part], wbuf.at[me, part], s_send.at[0, p], s_recv.at[0, p], sibling, t
            )
        slot = ring_slot(way, s)
        part = span(way, s, p)
        at = 1 + way * half_ring + s - 1
        return remote(
            wbuf.at[slot, part], wbuf.at[slot, part], s_send.at[at, p], s_recv.at[at, p], sibling, t
        )

    def sib_recv(way, s, p):
        if s == 0:
            slot, at, part = sibling, 0, span(0, 0, p)
        else:
            slot = ring_slot(way, s) - core + 1 - core
            at = 1 + way * half_ring + s - 1
            part = span(way, s, p)
        return remote(
            wbuf.at[slot, part], wbuf.at[slot, part], s_send.at[at, p], s_recv.at[at, p], sibling, t
        )

    @pl.loop(0, PIECES)
    def _(p):
        ring_send(0, 1, p).start()
        ring_send(1, 1, p).start()

    def grad_copy(k):
        return remote(
            grad, gbuf.at[t], g_send.at[k], g_recv.at[k], me, (t + k) % nt
        )

    def grad_recv(k):
        src = (t - k + nt) % nt
        return remote(grad, gbuf.at[src], g_send.at[k], g_recv.at[k], me, (t + k) % nt)

    for k in range(1, nt):
        grad_copy(k).start()

    locals_ = [
        pltpu.make_async_copy(acts, acts_v, local_sem.at[0]),
        pltpu.make_async_copy(proj_in, pin_v, local_sem.at[1]),
        pltpu.make_async_copy(proj_out, pout_v, local_sem.at[2]),
        pltpu.make_async_copy(weight, wbuf.at[me], local_sem.at[3]),
        pltpu.make_async_copy(gate, gate_v, local_sem.at[4]),
        pltpu.make_async_copy(up, up_v, local_sem.at[5]),
        pltpu.make_async_copy(grad, gbuf.at[t], local_sem.at[6]),
    ]
    for copy in locals_:
        copy.start()

    @pl.loop(0, PIECES)
    def _(p):
        sib_send(0, 0, p).start()

    locals_[0].wait()
    locals_[1].wait()
    iacc[...] = dot_nt(pin_v[...], acts_v[...])

    def in_copy(k):
        return remote(iacc, irecv.at[k - 1], i_send.at[k], i_recv.at[k], me, (t + k) % nt)

    for k in range(1, nt):
        in_copy(k).start()
    locals_[2].wait()
    per_t = ko // nt
    row_id = lax.broadcasted_iota(jnp.int32, (ko, ko), 0)
    col_id = lax.broadcasted_iota(jnp.int32, (ko, ko), 1)
    place = (col_id // per_t) * per_t + (col_id % 2) * tiles + (col_id % per_t) // 2
    pout_t[...] = jnp.dot(
        (row_id == place).astype(jnp.bfloat16), pout_v[...], preferred_element_type=jnp.float32
    ).astype(jnp.bfloat16)
    acc[...] = jnp.zeros_like(acc)
    inpad[...] = jnp.zeros_like(inpad)

    if half_ring > 1:
        @pl.loop(0, PIECES)
        def _(p):
            for s in range(1, half_ring):
                for way in (0, 1):
                    ring_recv(way, s, p).wait_recv()
                    ring_send(way, s + 1, p).start()
                    sib_send(way, s, p).start()

    for copy in locals_[3:]:
        copy.wait()
    for k in range(1, nt):
        grad_recv(k).wait_recv()
        in_copy(k).wait_recv()
    total_in = iacc[...]
    for k in range(1, nt):
        total_in = total_in + irecv[k - 1]
    inpad[0, 0:ki] = total_in
    inpad[1, ki : 2 * ki] = total_in

    @pl.loop(0, PIECES)
    def _(p):
        for way in (0, 1):
            ring_recv(way, half_ring, p).wait_recv()
            sib_send(way, half_ring, p).start()
        sib_recv(0, 0, p).wait_recv()
        for s in range(1, half_ring + 1):
            for way in (0, 1):
                sib_recv(way, s, p).wait_recv()
        here = pl.ds(pl.multiple_of(p * rows, LANES), rows)
        hidden = jnp.zeros((tokens, rows), jnp.float32)
        for j in range(n):
            at = j * kw
            hidden = hidden + dot_nt(
                gbuf[at // gw, :, at % gw : at % gw + kw], wbuf[j, here, :]
            )
        value = gate_v[:, here].astype(jnp.float32)
        sigma = jax.nn.sigmoid(value)
        slope = sigma + value * sigma * (1.0 - sigma)
        grads = (hidden * up_v[:, here].astype(jnp.float32) * slope).astype(jnp.bfloat16)
        acc[...] += dot_nt(pout_t[:, here], grads)

    for tt in range(nt):
        for par in (0, 1):
            first = (tt * 2 + par) * tiles
            oacc[tt, par] = acc[first : first + tiles, :]

    def out_copy(k):
        to = (t + k) % nt
        return remote(oacc.at[to], orecv.at[k - 1], o_send.at[k], o_recv.at[k], me, to)

    for k in range(1, nt):
        out_copy(k).start()
    for k in range(1, nt):
        out_copy(k).wait_recv()
    evens = oacc[t, 0]
    odds = oacc[t, 1]
    for k in range(1, nt):
        evens = evens + orecv[k - 1, 0]
        odds = odds + orecv[k - 1, 1]

    position = lax.broadcasted_iota(jnp.int32, (tiles, seq), 1)
    for e in range(ex):
        live = (position < lengths[e]).astype(jnp.float32)
        own = slice(e * seq, (e + 1) * seq)
        fbuf[me * ex + e] = dot_nt(evens[:, own] * live, inpad[0, :, own], HIGHEST) + dot_nt(
            odds[:, own] * live, inpad[1, :, own], HIGHEST
        )

    def feat_copy(k):
        part = fbuf.at[pl.ds(me * ex, ex)]
        return remote(part, part, f_send.at[k], f_recv.at[k], (me + k) % n, t)

    def feat_recv(k):
        part = fbuf.at[pl.ds(((me - k + n) % n) * ex, ex)]
        return remote(part, part, f_send.at[k], f_recv.at[k], (me + k) % n, t)

    for k in range(1, n):
        feat_copy(k).start()
    for k in range(1, n):
        feat_recv(k).wait_recv()

    for s in range(tiles):
        cols[s] = fbuf[:, s, :]

    owner = (me * row_tiles) // tiles
    offset = (me * row_tiles) % tiles

    def row_copy(k):
        return remote(
            cols.at[pl.ds(offset, row_tiles)], rbuf, r_send.at[k], r_recv, me, (t + k) % nt
        )

    @pl.when(t == owner)
    def _():
        for k in range(1, nt):
            row_copy(k).start()
        rbuf[...] = cols[pl.ds(offset, row_tiles)]

    inner = jnp.zeros((every, every), jnp.float32)
    for s in range(tiles):
        inner = inner + dot_nt(cols[s], cols[s], HIGHEST)
    kbuf[t] = jnp.zeros(kbuf.shape[1:], jnp.float32)
    kbuf[t, :, 0:every] = inner

    def inner_copy(k):
        return remote(kbuf.at[t], kbuf.at[t], k_send.at[k], k_recv.at[k], me, (t + k) % nt)

    def inner_recv(k):
        src = (t - k + nt) % nt
        return remote(kbuf.at[src], kbuf.at[src], k_send.at[k], k_recv.at[k], me, (t + k) % nt)

    for k in range(1, nt):
        inner_copy(k).start()

    for k in range(1, nt):
        inner_recv(k).wait_recv()
    whole = kbuf[0]
    for tt in range(1, nt):
        whole = whole + kbuf[tt]
    inner_out[...] = whole

    @pl.when(t != owner)
    def _():
        row_copy(1).wait_recv()

    @pl.loop(0, PIECES)
    def _(p):
        sib_send(0, 0, p).wait_send()
        for s in range(1, half_ring + 1):
            for way in (0, 1):
                ring_send(way, s, p).wait_send()
                sib_send(way, s, p).wait_send()

    for k in range(1, nt):
        grad_copy(k).wait_send()
        in_copy(k).wait_send()
        out_copy(k).wait_send()
        inner_copy(k).wait_send()
    for k in range(1, n):
        feat_copy(k).wait_send()

    @pl.when(t == owner)
    def _():
        for k in range(1, nt):
            row_copy(k).wait_send()


def finish(cols, rbuf, inner, query_ids, gram, scores, rhs_s, lhs_s, left_s, scale_s):
    tiles, every = cols.shape[0], cols.shape[1]
    step = pl.program_id(0)

    @pl.when(step == 0)
    def _():
        for s in range(tiles):
            value = cols[s]
            high = value.astype(jnp.bfloat16).astype(jnp.float32)
            own = slice(s * LANES, (s + 1) * LANES)
            lhs_s[0:every, own] = high
            lhs_s[every : 2 * every, own] = value - high
            lhs_s[2 * every : 3 * every, own] = high
        rhs_s[...] = lhs_s[...].astype(jnp.bfloat16)
        whole = inner[:, 0:every]
        r_id = lax.broadcasted_iota(jnp.int32, (every, every), 0)
        c_id = lax.broadcasted_iota(jnp.int32, (every, every), 1)
        norm_mean = jnp.sum(jnp.where(r_id == c_id, whole, 0.0)) / every + 1e-6
        ex, queries = scores.shape
        q_row = lax.broadcasted_iota(jnp.int32, (queries, every), 0)
        q_col = lax.broadcasted_iota(jnp.int32, (queries, every), 1)
        chosen = jnp.zeros((queries, every), jnp.float32)
        for q in range(queries):
            chosen = jnp.where((q_row == q) & (q_col == query_ids[q]), 1.0, chosen)
        e_row = lax.broadcasted_iota(jnp.int32, (ex, every), 0)
        e_col = lax.broadcasted_iota(jnp.int32, (ex, every), 1)
        mine = (e_col == e_row + lax.axis_index("dp") * ex).astype(jnp.float32)
        picked = jnp.dot(mine, whole, precision=HIGHEST, preferred_element_type=jnp.float32)
        scores[...] = dot_nt(picked, chosen, HIGHEST) / norm_mean
        width = tiles * LANES * lax.axis_size("tensor")
        scale_s[0] = (width / every) / norm_mean

    value = rbuf[step]
    high = value.astype(jnp.bfloat16).astype(jnp.float32)
    left_s[0:every, :] = high
    left_s[every : 2 * every, :] = high
    left_s[2 * every : 3 * every, :] = value - high
    left = left_s[...].T.astype(jnp.bfloat16)
    product = jnp.dot(left, rhs_s[...], preferred_element_type=jnp.float32)
    gram[...] = product * scale_s[0]


def body(n, nt, acts, grad_out, gate_pre, up_pre, down_weight, proj_in, proj_out, lengths, query_ids):
    tokens, gw = grad_out.shape
    ff, kw = down_weight.shape
    ki = proj_in.shape[1]
    ko = proj_out.shape[1]
    ex = lengths.shape[0]
    every = ex * n
    width = ki * ko
    tiles = width // nt // LANES
    row_tiles = width // n // LANES
    half_ring = n // 4
    bf16, f32 = jnp.bfloat16, jnp.float32
    dma = pltpu.SemaphoreType.DMA
    hbm = pl.BlockSpec(memory_space=pl.ANY)
    smem = pl.BlockSpec(memory_space=pltpu.SMEM)
    vmem = pl.BlockSpec(memory_space=pltpu.VMEM)
    cols, rows, inner = pl.pallas_call(
        functools.partial(kernel, n, nt),
        out_shape=(
            jax.ShapeDtypeStruct((tiles, every, LANES), f32),
            jax.ShapeDtypeStruct((row_tiles, every, LANES), f32),
            jax.ShapeDtypeStruct((every, LANES), f32),
        ),
        in_specs=[hbm] * 7 + [smem],
        out_specs=(vmem, vmem, vmem),
        scratch_shapes=[
            pltpu.VMEM((n, ff, kw), bf16),
            pltpu.VMEM((nt, tokens, gw), bf16),
            pltpu.VMEM((tokens, ff), bf16),
            pltpu.VMEM((tokens, ff), bf16),
            pltpu.VMEM((tokens, gw), bf16),
            pltpu.VMEM((ki, gw), bf16),
            pltpu.VMEM((ko, ff), bf16),
            pltpu.VMEM((ko, ff), bf16),
            pltpu.VMEM((ko, tokens), f32),
            pltpu.VMEM((nt, 2, tiles, tokens), f32),
            pltpu.VMEM((nt - 1, 2, tiles, tokens), f32),
            pltpu.VMEM((ki, tokens), f32),
            pltpu.VMEM((nt - 1, ki, tokens), f32),
            pltpu.VMEM((2, 2 * ki, tokens), f32),
            pltpu.VMEM((every, tiles, LANES), f32),
            pltpu.VMEM((nt, every, LANES), f32),
            dma((7,)),
            dma((2, half_ring, PIECES)),
            dma((2, half_ring, PIECES)),
            dma((1 + 2 * half_ring, PIECES)),
            dma((1 + 2 * half_ring, PIECES)),
            dma((nt,)), dma((nt,)), dma((nt,)), dma((nt,)), dma((nt,)), dma((nt,)),
            dma((n,)), dma((n,)),
            dma((nt,)), dma((nt,)),
            dma((nt,)), dma,
        ],
        compiler_params=pltpu.CompilerParams(
            collective_id=0, has_side_effects=True, vmem_limit_bytes=60 * 1024 * 1024
        ),
    )(acts, grad_out, gate_pre, up_pre, down_weight, proj_in.T, proj_out.T, lengths)
    gram, scores = pl.pallas_call(
        finish,
        grid=(row_tiles,),
        out_shape=(
            jax.ShapeDtypeStruct((width // n, width // nt), f32),
            jax.ShapeDtypeStruct((ex, query_ids.shape[0]), f32),
        ),
        in_specs=[
            pl.BlockSpec((tiles, every, LANES), lambda i: (0, 0, 0)),
            pl.BlockSpec((row_tiles, every, LANES), lambda i: (0, 0, 0)),
            pl.BlockSpec((every, LANES), lambda i: (0, 0)),
            smem,
        ],
        out_specs=(
            pl.BlockSpec((LANES, width // nt), lambda i: (i, 0)),
            pl.BlockSpec((ex, query_ids.shape[0]), lambda i: (0, 0)),
        ),
        scratch_shapes=[
            pltpu.VMEM((3 * every, tiles * LANES), bf16),
            pltpu.VMEM((3 * every, tiles * LANES), f32),
            pltpu.VMEM((3 * every, LANES), f32),
            pltpu.SMEM((1,), f32),
        ],
    )(cols, rows, inner, query_ids)
    return gram, scores.T


def solution(mesh):
    in_specs = (
        P("dp", "tensor"),
        P("dp", "tensor"),
        P("dp", "tensor"),
        P("dp", "tensor"),
        P("tensor", "dp"),
        P("tensor", None),
        P("tensor", None),
        P("dp"),
        P(),
    )
    out_specs = (P("dp", "tensor"), P(None, "dp"))
    return jax.shard_map(
        functools.partial(body, mesh.shape["dp"], mesh.shape["tensor"]),
        mesh=mesh, in_specs=in_specs, out_specs=out_specs, check_vma=False,
    )
```

```python
import functools

import jax
import jax.numpy as jnp
from jax import lax
from jax.experimental import pallas as pl
from jax.experimental.pallas import tpu as pltpu
from jax.sharding import PartitionSpec as P

MESH = pl.DeviceIdType.MESH
HIGHEST = lax.Precision.HIGHEST
LANES = 128
PIECES = 7


def dot_nt(a, b, precision=None):
    return lax.dot_general(
        a, b, (((1,), (1,)), ((), ())), preferred_element_type=jnp.float32, precision=precision
    )


def kernel(
    n, nt,
    acts, grad, gate, up, weight, proj_in, proj_out, lengths,
    rhs, rbuf, inner_out,
    wbuf, gbuf, gate_v, up_v, acts_v, pin_v, pout_v, pout_t,
    acc, oacc, orecv, iacc, irecv, inpad, fbuf, kbuf, cols, rhs_s,
    local_sem, w_send, w_recv, s_send, s_recv, g_send, g_recv, i_send, i_recv,
    o_send, o_recv, f_send, f_recv, k_send, k_recv, r_send, r_recv,
):
    me = lax.axis_index("dp")
    t = lax.axis_index("tensor")
    chips = n // 2
    half_ring = chips // 2
    chip = me // 2
    core = me % 2
    ff, kw = weight.shape
    tokens, gw = grad.shape
    ex = lengths.shape[0]
    seq = tokens // ex
    ki = proj_in.shape[0]
    ko = proj_out.shape[0]
    tiles = cols.shape[0]
    every = cols.shape[1]
    row_tiles = rbuf.shape[0]
    rows = ff // PIECES
    sibling = chip * 2 + 1 - core

    def step_left(c, s):
        if chips == 4:
            return [c, (3 * c + 2) % 5, 3 - c, (2 * c + 1) % 5][s % 4]
        return (c - s + chips) % chips

    def step_right(c, s):
        return step_left(c, chips - s)

    barrier = pltpu.get_barrier_semaphore()
    for k in range(1, n):
        pl.semaphore_signal(barrier, inc=1, device_id=((me + k) % n, t), device_id_type=MESH)
    for k in range(1, nt):
        pl.semaphore_signal(barrier, inc=1, device_id=(me, (t + k) % nt), device_id_type=MESH)
    pl.semaphore_wait(barrier, n + nt - 2)

    def remote(src, dst, send, recv, dp_id, t_id):
        return pltpu.make_async_remote_copy(
            src_ref=src, dst_ref=dst, send_sem=send, recv_sem=recv,
            device_id=(dp_id, t_id), device_id_type=MESH,
        )

    def span(way, s, p):
        if s < half_ring:
            return pl.ds(pl.multiple_of(p * rows, 32), rows)
        return pl.ds(pl.multiple_of(p * rows + way * (rows // 2), 32), rows // 2)

    def ring_send(way, s, p):
        origin = step_left(chip, s - 1) if way == 0 else step_right(chip, s - 1)
        target = step_right(chip, 1) if way == 0 else step_left(chip, 1)
        slot = origin * 2 + core
        part = span(way, s, p)
        src = weight.at[part] if s == 1 else wbuf.at[slot, part]
        return remote(
            src, wbuf.at[slot, part], w_send.at[way, s - 1, p], w_recv.at[way, s - 1, p],
            target * 2 + core, t,
        )

    def ring_slot(way, s):
        return (step_left(chip, s) if way == 0 else step_right(chip, s)) * 2 + core

    def ring_recv(way, s, p):
        slot = ring_slot(way, s)
        part = span(way, s, p)
        return remote(
            wbuf.at[slot, part], wbuf.at[slot, part],
            w_send.at[way, s - 1, p], w_recv.at[way, s - 1, p], sibling, t,
        )

    def sib_send(way, s, p):
        if s == 0:
            part = span(0, 0, p)
            return remote(
                weight.at[part], wbuf.at[me, part], s_send.at[0, p], s_recv.at[0, p], sibling, t
            )
        slot = ring_slot(way, s)
        part = span(way, s, p)
        at = 1 + way * half_ring + s - 1
        return remote(
            wbuf.at[slot, part], wbuf.at[slot, part], s_send.at[at, p], s_recv.at[at, p], sibling, t
        )

    def sib_recv(way, s, p):
        if s == 0:
            slot, at, part = sibling, 0, span(0, 0, p)
        else:
            slot = ring_slot(way, s) - core + 1 - core
            at = 1 + way * half_ring + s - 1
            part = span(way, s, p)
        return remote(
            wbuf.at[slot, part], wbuf.at[slot, part], s_send.at[at, p], s_recv.at[at, p], sibling, t
        )

    @pl.loop(0, PIECES)
    def _(p):
        ring_send(0, 1, p).start()
        ring_send(1, 1, p).start()

    def grad_copy(k):
        return remote(
            grad, gbuf.at[t], g_send.at[k], g_recv.at[k], me, (t + k) % nt
        )

    def grad_recv(k):
        src = (t - k + nt) % nt
        return remote(grad, gbuf.at[src], g_send.at[k], g_recv.at[k], me, (t + k) % nt)

    for k in range(1, nt):
        grad_copy(k).start()

    locals_ = [
        pltpu.make_async_copy(acts, acts_v, local_sem.at[0]),
        pltpu.make_async_copy(proj_in, pin_v, local_sem.at[1]),
        pltpu.make_async_copy(proj_out, pout_v, local_sem.at[2]),
        pltpu.make_async_copy(weight, wbuf.at[me], local_sem.at[3]),
        pltpu.make_async_copy(gate, gate_v, local_sem.at[4]),
        pltpu.make_async_copy(up, up_v, local_sem.at[5]),
        pltpu.make_async_copy(grad, gbuf.at[t], local_sem.at[6]),
    ]
    for copy in locals_:
        copy.start()

    @pl.loop(0, PIECES)
    def _(p):
        sib_send(0, 0, p).start()

    locals_[0].wait()
    locals_[1].wait()
    iacc[...] = dot_nt(pin_v[...], acts_v[...])

    def in_copy(k):
        return remote(iacc, irecv.at[k - 1], i_send.at[k], i_recv.at[k], me, (t + k) % nt)

    for k in range(1, nt):
        in_copy(k).start()
    locals_[2].wait()
    per_t = ko // nt
    row_id = lax.broadcasted_iota(jnp.int32, (ko, ko), 0)
    col_id = lax.broadcasted_iota(jnp.int32, (ko, ko), 1)
    place = (col_id // per_t) * per_t + (col_id % 2) * tiles + (col_id % per_t) // 2
    pout_t[...] = jnp.dot(
        (row_id == place).astype(jnp.bfloat16), pout_v[...], preferred_element_type=jnp.float32
    ).astype(jnp.bfloat16)
    acc[...] = jnp.zeros_like(acc)
    inpad[...] = jnp.zeros_like(inpad)

    if half_ring > 1:
        @pl.loop(0, PIECES)
        def _(p):
            for s in range(1, half_ring):
                for way in (0, 1):
                    ring_recv(way, s, p).wait_recv()
                    ring_send(way, s + 1, p).start()
                    sib_send(way, s, p).start()

    for copy in locals_[3:]:
        copy.wait()
    for k in range(1, nt):
        grad_recv(k).wait_recv()
        in_copy(k).wait_recv()
    total_in = iacc[...]
    for k in range(1, nt):
        total_in = total_in + irecv[k - 1]
    inpad[0, 0:ki] = total_in
    inpad[1, ki : 2 * ki] = total_in

    @pl.loop(0, PIECES)
    def _(p):
        here = pl.ds(pl.multiple_of(p * rows, LANES), rows)

        def product(slot):
            at = slot * kw
            own = pl.ds(pl.multiple_of(at % gw, LANES), kw)
            return dot_nt(gbuf[at // gw, :, own], wbuf[slot, here, :])

        sib_recv(0, 0, p).wait_recv()
        for s in range(1, half_ring):
            for way in (0, 1):
                sib_recv(way, s, p).wait_recv()
        hidden = product(me) + product(sibling)
        for s in range(1, half_ring):
            for way in (0, 1):
                slot = ring_slot(way, s)
                hidden = hidden + product(slot) + product(slot - core + 1 - core)
        for way in (0, 1):
            ring_recv(way, half_ring, p).wait_recv()
            sib_send(way, half_ring, p).start()
        far = ring_slot(0, half_ring)
        hidden = hidden + product(far)
        for way in (0, 1):
            sib_recv(way, half_ring, p).wait_recv()
        hidden = hidden + product(far - core + 1 - core)
        value = gate_v[:, here].astype(jnp.float32)
        sigma = jax.nn.sigmoid(value)
        slope = sigma + value * sigma * (1.0 - sigma)
        grads = (hidden * up_v[:, here].astype(jnp.float32) * slope).astype(jnp.bfloat16)
        acc[...] += dot_nt(pout_t[:, here], grads)

    for tt in range(nt):
        for par in (0, 1):
            first = (tt * 2 + par) * tiles
            oacc[tt, par] = acc[first : first + tiles, :]

    def out_copy(k):
        to = (t + k) % nt
        return remote(oacc.at[to], orecv.at[k - 1], o_send.at[k], o_recv.at[k], me, to)

    for k in range(1, nt):
        out_copy(k).start()
    for k in range(1, nt):
        out_copy(k).wait_recv()
    evens = oacc[t, 0]
    odds = oacc[t, 1]
    for k in range(1, nt):
        evens = evens + orecv[k - 1, 0]
        odds = odds + orecv[k - 1, 1]

    position = lax.broadcasted_iota(jnp.int32, (tiles, seq), 1)
    for e in range(ex):
        live = (position < lengths[e]).astype(jnp.float32)
        own = slice(e * seq, (e + 1) * seq)
        fbuf[me * ex + e] = dot_nt(evens[:, own] * live, inpad[0, :, own], HIGHEST) + dot_nt(
            odds[:, own] * live, inpad[1, :, own], HIGHEST
        )

    def feat_copy(k):
        part = fbuf.at[pl.ds(me * ex, ex)]
        return remote(part, part, f_send.at[k], f_recv.at[k], (me + k) % n, t)

    def feat_recv(k):
        part = fbuf.at[pl.ds(((me - k + n) % n) * ex, ex)]
        return remote(part, part, f_send.at[k], f_recv.at[k], (me + k) % n, t)

    for k in range(1, n):
        feat_copy(k).start()
    for k in range(1, n):
        feat_recv(k).wait_recv()

    for s in range(tiles):
        cols[s] = fbuf[:, s, :]

    owner = (me * row_tiles) // tiles
    offset = (me * row_tiles) % tiles

    def row_copy(k):
        return remote(
            cols.at[pl.ds(offset, row_tiles)], rbuf, r_send.at[k], r_recv, me, (t + k) % nt
        )

    @pl.when(t == owner)
    def _():
        for k in range(1, nt):
            row_copy(k).start()
        rbuf[...] = cols[pl.ds(offset, row_tiles)]

    inner = jnp.zeros((every, every), jnp.float32)
    for s in range(tiles):
        inner = inner + dot_nt(cols[s], cols[s], HIGHEST)
    kbuf[t] = jnp.zeros(kbuf.shape[1:], jnp.float32)
    kbuf[t, :, 0:every] = inner

    def inner_copy(k):
        return remote(kbuf.at[t], kbuf.at[t], k_send.at[k], k_recv.at[k], me, (t + k) % nt)

    def inner_recv(k):
        src = (t - k + nt) % nt
        return remote(kbuf.at[src], kbuf.at[src], k_send.at[k], k_recv.at[k], me, (t + k) % nt)

    for k in range(1, nt):
        inner_copy(k).start()

    for s in range(tiles):
        value = cols[s]
        high = value.astype(jnp.bfloat16).astype(jnp.float32)
        own = slice(s * LANES, (s + 1) * LANES)
        rhs_s[0:every, own] = high
        rhs_s[every : 2 * every, own] = value - high
        rhs_s[2 * every : 3 * every, own] = high
    rhs[...] = rhs_s[...].astype(jnp.bfloat16)

    for k in range(1, nt):
        inner_recv(k).wait_recv()
    whole = kbuf[0]
    for tt in range(1, nt):
        whole = whole + kbuf[tt]
    inner_out[...] = whole

    @pl.when(t != owner)
    def _():
        row_copy(1).wait_recv()

    @pl.loop(0, PIECES)
    def _(p):
        sib_send(0, 0, p).wait_send()
        for s in range(1, half_ring + 1):
            for way in (0, 1):
                ring_send(way, s, p).wait_send()
                sib_send(way, s, p).wait_send()

    for k in range(1, nt):
        grad_copy(k).wait_send()
        in_copy(k).wait_send()
        out_copy(k).wait_send()
        inner_copy(k).wait_send()
    for k in range(1, n):
        feat_copy(k).wait_send()

    @pl.when(t == owner)
    def _():
        for k in range(1, nt):
            row_copy(k).wait_send()


def finish(rhs, rbuf, inner, query_ids, gram, scores, left_s, scale_s):
    every = inner.shape[0]
    step = pl.program_id(0)

    @pl.when(step == 0)
    def _():
        whole = inner[:, 0:every]
        r_id = lax.broadcasted_iota(jnp.int32, (every, every), 0)
        c_id = lax.broadcasted_iota(jnp.int32, (every, every), 1)
        norm_mean = jnp.sum(jnp.where(r_id == c_id, whole, 0.0)) / every + 1e-6
        ex, queries = scores.shape
        q_row = lax.broadcasted_iota(jnp.int32, (queries, every), 0)
        q_col = lax.broadcasted_iota(jnp.int32, (queries, every), 1)
        chosen = jnp.zeros((queries, every), jnp.float32)
        for q in range(queries):
            chosen = jnp.where((q_row == q) & (q_col == query_ids[q]), 1.0, chosen)
        e_row = lax.broadcasted_iota(jnp.int32, (ex, every), 0)
        e_col = lax.broadcasted_iota(jnp.int32, (ex, every), 1)
        mine = (e_col == e_row + lax.axis_index("dp") * ex).astype(jnp.float32)
        picked = jnp.dot(mine, whole, precision=HIGHEST, preferred_element_type=jnp.float32)
        scores[...] = dot_nt(picked, chosen, HIGHEST) / norm_mean
        width = rhs.shape[1] * lax.axis_size("tensor")
        scale_s[0] = (width / every) / norm_mean

    value = rbuf[step]
    high = value.astype(jnp.bfloat16).astype(jnp.float32)
    left_s[0:every, :] = high
    left_s[every : 2 * every, :] = high
    left_s[2 * every : 3 * every, :] = value - high
    left = left_s[...].T.astype(jnp.bfloat16)
    product = jnp.dot(left, rhs[...], preferred_element_type=jnp.float32)
    gram[...] = product * scale_s[0]


def body(n, nt, acts, grad_out, gate_pre, up_pre, down_weight, proj_in, proj_out, lengths, query_ids):
    tokens, gw = grad_out.shape
    ff, kw = down_weight.shape
    ki = proj_in.shape[1]
    ko = proj_out.shape[1]
    ex = lengths.shape[0]
    every = ex * n
    width = ki * ko
    tiles = width // nt // LANES
    row_tiles = width // n // LANES
    half_ring = n // 4
    bf16, f32 = jnp.bfloat16, jnp.float32
    dma = pltpu.SemaphoreType.DMA
    hbm = pl.BlockSpec(memory_space=pl.ANY)
    smem = pl.BlockSpec(memory_space=pltpu.SMEM)
    vmem = pl.BlockSpec(memory_space=pltpu.VMEM)
    rhs, rows, inner = pl.pallas_call(
        functools.partial(kernel, n, nt),
        out_shape=(
            jax.ShapeDtypeStruct((3 * every, tiles * LANES), bf16),
            jax.ShapeDtypeStruct((row_tiles, every, LANES), f32),
            jax.ShapeDtypeStruct((every, LANES), f32),
        ),
        in_specs=[hbm] * 7 + [smem],
        out_specs=(vmem, vmem, vmem),
        scratch_shapes=[
            pltpu.VMEM((n, ff, kw), bf16),
            pltpu.VMEM((nt, tokens, gw), bf16),
            pltpu.VMEM((tokens, ff), bf16),
            pltpu.VMEM((tokens, ff), bf16),
            pltpu.VMEM((tokens, gw), bf16),
            pltpu.VMEM((ki, gw), bf16),
            pltpu.VMEM((ko, ff), bf16),
            pltpu.VMEM((ko, ff), bf16),
            pltpu.VMEM((ko, tokens), f32),
            pltpu.VMEM((nt, 2, tiles, tokens), f32),
            pltpu.VMEM((nt - 1, 2, tiles, tokens), f32),
            pltpu.VMEM((ki, tokens), f32),
            pltpu.VMEM((nt - 1, ki, tokens), f32),
            pltpu.VMEM((2, 2 * ki, tokens), f32),
            pltpu.VMEM((every, tiles, LANES), f32),
            pltpu.VMEM((nt, every, LANES), f32),
            pltpu.VMEM((tiles, every, LANES), f32),
            pltpu.VMEM((3 * every, tiles * LANES), f32),
            dma((7,)),
            dma((2, half_ring, PIECES)),
            dma((2, half_ring, PIECES)),
            dma((1 + 2 * half_ring, PIECES)),
            dma((1 + 2 * half_ring, PIECES)),
            dma((nt,)), dma((nt,)), dma((nt,)), dma((nt,)), dma((nt,)), dma((nt,)),
            dma((n,)), dma((n,)),
            dma((nt,)), dma((nt,)),
            dma((nt,)), dma,
        ],
        compiler_params=pltpu.CompilerParams(
            collective_id=0, has_side_effects=True, vmem_limit_bytes=60 * 1024 * 1024
        ),
    )(acts, grad_out, gate_pre, up_pre, down_weight, proj_in.T, proj_out.T, lengths)
    gram, scores = pl.pallas_call(
        finish,
        grid=(row_tiles,),
        out_shape=(
            jax.ShapeDtypeStruct((width // n, width // nt), f32),
            jax.ShapeDtypeStruct((ex, query_ids.shape[0]), f32),
        ),
        in_specs=[
            pl.BlockSpec((3 * every, tiles * LANES), lambda i: (0, 0)),
            pl.BlockSpec((row_tiles, every, LANES), lambda i: (0, 0, 0)),
            pl.BlockSpec((every, LANES), lambda i: (0, 0)),
            smem,
        ],
        out_specs=(
            pl.BlockSpec((LANES, width // nt), lambda i: (i, 0)),
            pl.BlockSpec((ex, query_ids.shape[0]), lambda i: (0, 0)),
        ),
        scratch_shapes=[
            pltpu.VMEM((3 * every, LANES), f32),
            pltpu.SMEM((1,), f32),
        ],
    )(rhs, rows, inner, query_ids)
    return gram, scores.T


def solution(mesh):
    in_specs = (
        P("dp", "tensor"),
        P("dp", "tensor"),
        P("dp", "tensor"),
        P("dp", "tensor"),
        P("tensor", "dp"),
        P("tensor", None),
        P("tensor", None),
        P("dp"),
        P(),
    )
    out_specs = (P("dp", "tensor"), P(None, "dp"))
    return jax.shard_map(
        functools.partial(body, mesh.shape["dp"], mesh.shape["tensor"]),
        mesh=mesh, in_specs=in_specs, out_specs=out_specs, check_vma=False,
    )
```
